32 devices in a mesh: lat: 4 (over x, core), lon: 8 (over z, y).
Axes of the slice: x: 2, y: 2, z: 4, core: 2. Of those that a mesh axis runs over, the one named last changes fastest.
Arguments:
- ensemble: bfloat16 [80, 8, 32, 1024], P(None, None, 'lat', 'lon'), may hold values from -6 to 6
- static_sigma: float32 [8], replicated, may hold values from 0.5 to 2
- lat_taps: float32 [17], replicated, may hold values from 0.01 to 0.12
- lon_taps: float32 [17], replicated, may hold values from 0.01 to 0.12
- step_len: float32 [2], replicated, may hold values from 0.2 to 0.6
- send_cols: int32 [4, 8, 32, 256], P('lat', 'lon'), may hold values from 0 to 1023
- send_count: int32 [4, 8, 32], P('lat', 'lon'), may hold values from 128 to 256, as said below
- obs_ref: int32 [4, 8, 4, 2048], P('lat', 'lon'), may hold values from 0 to 8191, as said below
- obs_level: int32 [4, 8, 2048], P('lat', 'lon'), may hold values from 0 to 7
- obs_weight: float32 [4, 8, 4, 2048], P('lat', 'lon'), may hold values from 0 to 1
- innovation: float32 [4, 8, 2048], P('lat', 'lon'), may hold values from -6 to 6
- obs_precision: float32 [4, 8, 2048], P('lat', 'lon'), may hold values from 0.25 to 1
Outputs:
- ens_control: float32 [80, 8, 32, 1024], P(None, None, 'lat', 'lon')
- static_control: float32 [8, 32, 1024], P(None, 'lat', 'lon')
- departures: float32 [4, 8, 2048], P('lat', 'lon')
The draws below stay inside these ranges and needn't reach their ends.
Inputs may be any that keep to these rules, and one draw needn't show every extreme that they name: `send_count`: number of leading slots of send_cols[a, b, e] that are live. One device receives 256 live slots from every device. `obs_ref`: position in the owning device's list L_e of received live columns; always below the total live slots that device receives.
All inputs are finite; a program needn't handle non-finite values.
Results may differ from the reference program's by a relative error of at most 0.0003.
Values may be sent and summed in bfloat16 or wider, within the bound.
A program may use at most 128 MiB of HBM per device.

```python
import math
import jax
import jax.numpy as jnp
from jax import lax

MEM = 80
LEV = 8
HW = 8
ITERS = 2
CLAT = 8
CLON = 128
NOBS_DEV = 2048
SLOT = 256
NLAT = 32
NLON = 1024
N_LAT = 4
N_LON = 8
DEVICES = 32


def count_table(key):
    table_key = jax.random.fold_in(key, 11)
    lead_key, hot_key = jax.random.split(table_key, 2)
    base_count = jax.random.randint(lead_key, (N_LAT, N_LON, DEVICES), SLOT // 2, SLOT + 1)
    hot_target = jax.random.randint(hot_key, (), 0, DEVICES)
    target = lax.broadcasted_iota(jnp.int32, (N_LAT, N_LON, DEVICES), 2)
    return jnp.where(target == hot_target, SLOT, base_count).astype(jnp.int32)


def draw_send_count(key, part):
    return count_table(key)


def draw_obs_ref(key, part):
    counts = count_table(key).reshape(DEVICES, DEVICES)
    totals = jnp.sum(counts, axis=0).reshape(N_LAT, N_LON, 1, 1)
    raw_draw = jax.random.randint(jax.random.fold_in(key, 23), (N_LAT, N_LON, 4, NOBS_DEV), 0, 2 ** 30)
    return (raw_draw % totals).astype(jnp.int32)


def place_ends(entries, stream_key, low, top_value):
    dims = entries.shape
    index_at = [jax.random.randint(jax.random.fold_in(stream_key, axis), (), 0, dims[axis]) for axis in range(len(dims))]
    entries = entries.at[tuple(index_at)].set(low)
    longest = dims.index(max(dims))
    index_at[longest] = (index_at[longest] + 1) % dims[longest]
    return entries.at[tuple(index_at)].set(top_value)


def shard_levels(stream_key, extent, cuts, smallest, top_value):
    def one(position, blocks):
        draws = jax.random.uniform(jax.random.fold_in(jax.random.fold_in(stream_key, 6), position), (blocks,), jnp.float32, smallest / len(cuts), top_value / len(cuts))
        return jnp.repeat(jnp.exp(draws), extent[position] // blocks).reshape((-1,) + (1,) * (len(extent) - position - 1))

    factor_of = one(*cuts[0])
    for cut in cuts[1:]:
        factor_of = factor_of * one(*cut)
    return factor_of


def scatter_about(stream_key, shape, width, bound, cuts=(), kind=jnp.bfloat16):
    values = width * jax.random.normal(stream_key, shape, jnp.float32)
    if cuts:
        values = values * shard_levels(stream_key, shape, cuts, -0.22, 0.18)
    return jnp.clip(values, -bound, bound).astype(kind)


def setup_inputs(seed: int = 0) -> dict:
    streams_of = jax.random.split(jax.random.key(seed), 13)
    ensemble = scatter_about(streams_of[0], (MEM, LEV, NLAT, NLON), 1.0, 6.0, ((2, 4), (3, 8)))
    static_sigma = jnp.clip(jnp.exp(jax.random.uniform(streams_of[1], (LEV,), jnp.float32, math.log(0.5), math.log(2.0))), 0.5, 2.0)
    lat_taps = jnp.clip(jnp.exp(jax.random.uniform(streams_of[2], (2 * HW + 1,), jnp.float32, math.log(0.01), math.log(0.12))), 0.01, 0.12)
    lon_taps = jnp.clip(jnp.exp(jax.random.uniform(streams_of[3], (2 * HW + 1,), jnp.float32, math.log(0.01), math.log(0.12))), 0.01, 0.12)
    step_len = jnp.clip(jax.random.uniform(streams_of[4], (ITERS,), jnp.float32, 0.2, 0.6), 0.2, 0.6)
    send_cols = place_ends(jax.random.randint(streams_of[5], (N_LAT, N_LON, DEVICES, SLOT), 0, CLAT * CLON), jax.random.fold_in(streams_of[5], 1), 0, (CLAT * CLON) - 1).astype(jnp.int32)
    send_count = draw_send_count(jax.random.fold_in(streams_of[12], 71), 0)
    obs_ref = draw_obs_ref(jax.random.fold_in(streams_of[12], 71), 0)
    obs_level = place_ends(jax.random.randint(streams_of[8], (N_LAT, N_LON, NOBS_DEV), 0, LEV), jax.random.fold_in(streams_of[8], 1), 0, LEV - 1).astype(jnp.int32)
    obs_weight = jnp.clip(1.0 * jax.random.uniform(streams_of[9], (N_LAT, N_LON, 4, NOBS_DEV), jnp.float32) ** shard_levels(streams_of[9], (N_LAT, N_LON, 4, NOBS_DEV), ((0, 4), (1, 8)), -0.2, 0.2), 0.0, 1.0)
    innovation = scatter_about(streams_of[10], (N_LAT, N_LON, NOBS_DEV), 1.0, 6.0, ((0, 4), (1, 8)), jnp.float32)
    obs_precision = jnp.clip(jnp.exp(math.log(1.0) - 1.3862944 * jax.random.uniform(streams_of[11], (N_LAT, N_LON, NOBS_DEV), jnp.float32) ** shard_levels(streams_of[11], (N_LAT, N_LON, NOBS_DEV), ((0, 4), (1, 8)), -0.2, 0.2)), 0.25, 1.0)
    return dict(ensemble=ensemble, static_sigma=static_sigma, lat_taps=lat_taps, lon_taps=lon_taps, step_len=step_len, send_cols=send_cols, send_count=send_count, obs_ref=obs_ref, obs_level=obs_level, obs_weight=obs_weight, innovation=innovation, obs_precision=obs_precision)


HYBRID_STATIC = 0.5
HYBRID_ENSEMBLE = 0.8660254037844386

def smooth_whole(fields, lat_taps, lon_taps):
    half_width = (lat_taps.shape[0] - 1) // 2
    lat_count = fields.shape[1]
    padded = jnp.pad(fields, ((0, 0), (half_width, half_width), (0, 0)))
    lat_pass = jnp.zeros_like(fields)
    for offset in range(2 * half_width + 1):
        lat_pass = lat_pass + lat_taps[offset] * padded[:, offset:offset + lat_count, :]
    result = jnp.zeros_like(fields)
    for offset in range(2 * half_width + 1):
        result = result + lon_taps[offset] * jnp.roll(lat_pass, half_width - offset, axis=2)
    return result

def smooth_adjoint(fields, lat_taps, lon_taps):
    half_width = (lat_taps.shape[0] - 1) // 2
    lat_count = fields.shape[1]
    lat_flip = lat_taps[::-1]
    lon_flip = lon_taps[::-1]
    lon_pass = jnp.zeros_like(fields)
    for offset in range(2 * half_width + 1):
        lon_pass = lon_pass + lon_flip[offset] * jnp.roll(fields, half_width - offset, axis=2)
    padded = jnp.pad(lon_pass, ((0, 0), (half_width, half_width), (0, 0)))
    result = jnp.zeros_like(fields)
    for offset in range(2 * half_width + 1):
        result = result + lat_flip[offset] * padded[:, offset:offset + lat_count, :]
    return result

def reference(ensemble, static_sigma, lat_taps, lon_taps, step_len, send_cols, send_count, obs_ref, obs_level, obs_weight, innovation, obs_precision):
    device_count = N_LAT * N_LON
    slot_count = send_cols.shape[-1]
    members, level_count, lat_total, lon_total = ensemble.shape
    lat_rows = lat_total // N_LAT
    lon_cells = lon_total // N_LON
    counts = send_count.reshape(device_count, device_count)
    slot_ends = jnp.cumsum(counts, axis=0)
    column_table = send_cols.reshape(device_count, device_count, slot_count)
    positions = obs_ref.reshape(device_count, 4, -1)

    def locate(target):
        target_ends = slot_ends[:, target]
        source = jnp.searchsorted(target_ends, positions[target], side='right').astype(jnp.int32)
        first_slot = (target_ends - counts[:, target])[source]
        local_cell = column_table[source, target, positions[target] - first_slot]
        grid_row = source // N_LON * lat_rows + local_cell // lon_cells
        grid_col = source % N_LON * lon_cells + local_cell % lon_cells
        return (grid_row, grid_col)
    grid_rows, grid_cols = jax.vmap(locate)(jnp.arange(device_count, dtype=jnp.int32))
    levels = jnp.broadcast_to(obs_level.reshape(device_count, 1, -1), grid_rows.shape)
    weights = obs_weight.reshape(device_count, 4, -1)
    innovations = innovation.reshape(device_count, -1)
    precision_obs = obs_precision.reshape(device_count, -1)
    ens_scale = HYBRID_ENSEMBLE / math.sqrt(members - 1)
    sigma = static_sigma[:, None, None]
    control = jnp.zeros(ensemble.shape, jnp.float32)
    static = jnp.zeros((level_count, lat_total, lon_total), jnp.float32)
    departure = -innovations
    for iteration in range(ITERS):
        if iteration > 0:

            def accumulate(running, member_pair):
                member, member_control = member_pair
                return (running + member.astype(jnp.float32) * smooth_whole(member_control, lat_taps, lon_taps), None)
            ens_part, unused = lax.scan(accumulate, jnp.zeros((level_count, lat_total, lon_total), jnp.float32), (ensemble, control))
            increment = ens_scale * ens_part + HYBRID_STATIC * sigma * smooth_whole(static, lat_taps, lon_taps)
            departure = lax.optimization_barrier(jnp.sum(weights * increment[levels, grid_rows, grid_cols], axis=1)) - innovations
        forcing = jnp.zeros((level_count, lat_total, lon_total), jnp.float32).at[levels, grid_rows, grid_cols].add(weights * (precision_obs * departure)[:, None, :])
        adjoint = lax.map(lambda member: smooth_adjoint(member.astype(jnp.float32) * forcing, lat_taps, lon_taps), ensemble)
        control = control - step_len[iteration] * (ens_scale * adjoint + control)
        static = static - step_len[iteration] * (HYBRID_STATIC * sigma * smooth_adjoint(forcing, lat_taps, lon_taps) + static)
    return (control, static, departure.reshape(N_LAT, N_LON, -1))
```

```python
import functools
import math

import jax
import jax.numpy as jnp
from jax import lax
from jax.experimental import pallas as pl
from jax.experimental.pallas import tpu as pltpu
from jax.sharding import PartitionSpec as P

HYBRID_STATIC = 0.5
HYBRID_ENSEMBLE = 0.8660254037844386
BF16 = jnp.bfloat16
F32 = jnp.float32
VMEM = pl.BlockSpec(memory_space=pltpu.VMEM)


def halves(x):
    high = x.astype(BF16)
    return high, (x - high.astype(F32)).astype(BF16)


def dot(a, b):
    return jnp.dot(a, b, preferred_element_type=F32)


def dot_nt(a, b):
    return lax.dot_general(a, b, (((1,), (1,)), ((), ())), preferred_element_type=F32)


def dot3(a, b):
    a_high, a_low = halves(a)
    b_high, b_low = halves(b)
    return dot(a_high, b_high) + dot(a_high, b_low) + dot(a_low, b_high)


def iota(shape, dim):
    return lax.broadcasted_iota(jnp.int32, shape, dim)


def obs_kernel(picking, chunk, *refs):
    if picking:
        table, hi, lo, weight, innov, prec, departure, out = refs
        table_high, table_low = halves(table[...])
    else:
        hi, lo, weight, innov, prec, departure, out = refs
    rows, slots = out.shape
    points = hi.shape[0]
    out[...] = jnp.zeros_like(out)

    def step(index, carry):
        where = pl.ds(pl.multiple_of(index * chunk, chunk), chunk)
        row_ids = iota((rows, chunk), 0)
        slot_ids = iota((slots, chunk), 0)
        value = -innov[:, where]
        if picking:
            for q in range(points):
                lo_hot = jnp.where(slot_ids == lo[q : q + 1, where], 1.0, 0.0).astype(BF16)
                product = dot(table_high, lo_hot) + dot(table_low, lo_hot)
                picked = jnp.sum(
                    jnp.where(row_ids == hi[q : q + 1, where], product, 0.0), axis=0, keepdims=True
                )
                value = value + weight[q : q + 1, where] * picked
        departure[:, where] = value
        value = prec[:, where] * value
        total = None
        for q in range(points):
            lo_hot = jnp.where(slot_ids == lo[q : q + 1, where], 1.0, 0.0).astype(BF16)
            pushed = weight[q : q + 1, where] * value
            high = pushed.astype(BF16).astype(F32)
            chosen = row_ids == hi[q : q + 1, where]
            term = dot_nt(jnp.where(chosen, high, 0.0).astype(BF16), lo_hot) + dot_nt(
                jnp.where(chosen, pushed - high, 0.0).astype(BF16), lo_hot
            )
            total = term if total is None else total + term
        out[...] += total
        return carry

    lax.fori_loop(0, hi.shape[1] // chunk, step, 0)


def observe(table, hi, lo, weight, innov, prec, rows, slots):
    operands = (hi, lo, weight, innov, prec)
    if table is not None:
        operands = (table,) + operands
    chunk = 512 if rows <= 256 else 256
    return pl.pallas_call(
        functools.partial(obs_kernel, table is not None, chunk),
        out_shape=(
            jax.ShapeDtypeStruct(innov.shape, F32),
            jax.ShapeDtypeStruct((rows, slots), F32),
        ),
        in_specs=[VMEM] * len(operands),
        out_specs=(VMEM, VMEM),
        name="observe",
    )(*operands)


def slots_kernel(cols, field, out):
    cells = field.shape[1]
    levels, width = out.shape[1:]
    lat_rows = field.shape[0] // levels
    both = jnp.concatenate(halves(field[...]), axis=0)

    def step(index, carry):
        col = cols[pl.ds(index, 1), :]
        cell_hot = jnp.where(iota((cells, width), 0) == col % cells, 1.0, 0.0).astype(BF16)
        product = dot(both, cell_hot)
        product = product[: field.shape[0]] + product[field.shape[0] :]
        row = jnp.broadcast_to(col // cells, (levels, width))
        total = jnp.zeros((levels, width), F32)
        for r in range(lat_rows):
            total = jnp.where(row == r, product[r * levels : (r + 1) * levels], total)
        out[index] = total
        return carry

    lax.fori_loop(0, cols.shape[0], step, 0, unroll=2)


def columns_kernel(cols, values, out):
    cells = out.shape[1]
    levels, width = values.shape[1:]
    lat_rows = out.shape[0] // levels

    def step(index, total):
        col = cols[pl.ds(index, 1), :]
        cell_hot = jnp.where(iota((cells, width), 0) == col % cells, 1.0, 0.0).astype(BF16)
        row = jnp.broadcast_to(col // cells, (levels, width))
        value = values[index]
        high = value.astype(BF16).astype(F32)
        parts = [jnp.where(row == r, high, 0.0) for r in range(lat_rows)]
        parts += [jnp.where(row == r, value - high, 0.0) for r in range(lat_rows)]
        return total + dot_nt(jnp.concatenate(parts, axis=0).astype(BF16), cell_hot)

    total = lax.fori_loop(
        0, cols.shape[0], step, jnp.zeros((2 * out.shape[0], cells), F32), unroll=2
    )
    out[...] = total[: out.shape[0]] + total[out.shape[0] :]


def covariance_kernel(blocks_lat, blocks_lon, coef, members, forcing, lat_op, lon_op, out, wide, mid):
    count = members.shape[1]
    rows, cells = forcing.shape[1:]
    height = blocks_lat * rows
    fields = count + 1
    for b in range(blocks_lon):
        for a in range(blocks_lat):
            spot = a * blocks_lon + b
            part = forcing[spot]
            for k in range(fields):
                piece = part if k == count else members[spot, k].astype(F32) * part
                at = pl.ds(k * height + a * rows, rows)
                wide[at, (b + 1) * cells : (b + 2) * cells] = piece
                if b == 0:
                    wide[at, (blocks_lon + 1) * cells :] = piece
                if b == blocks_lon - 1:
                    wide[at, :cells] = piece
    lon_high, lon_low = halves(lon_op[...])
    for b in range(blocks_lon):
        high, low = halves(wide[:, b * cells : (b + 3) * cells])
        mid[:, b * cells : (b + 1) * cells] = (
            dot(high, lon_high) + dot(high, lon_low) + dot(low, lon_high)
        )
    size = lat_op.shape[0]
    group = size // height
    for first in range(0, fields, group):
        where = pl.ds(first * height, size)
        wide[where, : blocks_lon * cells] = dot3(lat_op[...], mid[where, :])
    for a in range(blocks_lat):
        for b in range(blocks_lon):
            spot = a * blocks_lon + b
            total = coef[0] * wide[
                pl.ds(count * height + a * rows, rows), b * cells : (b + 1) * cells
            ]
            for k in range(count):
                total = total + coef[1] * (
                    members[spot, k].astype(F32)
                    * wide[pl.ds(k * height + a * rows, rows), b * cells : (b + 1) * cells]
                )
            out[spot] = total


def adjoint_kernel(scale, members, edges, field, sigma, lon_op, lat_op, out, static_out):
    batch, levels, rows, cells = out.shape
    lon_high, lon_low = halves(lon_op[...])

    def smooth(pieces, count):
        passes = []
        for piece in pieces:
            high, low = halves(piece)
            passes.append(
                (dot(high, lon_high) + dot(high, lon_low) + dot(low, lon_high)).reshape(
                    count, rows, cells
                )
            )
        stacked = jnp.concatenate(passes, axis=1)
        group = lat_op.shape[0] // rows
        results = []
        for first in range(0, count, group):
            results.append(
                dot3(
                    lat_op[...],
                    stacked[first : first + group].reshape(group * 3 * rows, cells),
                )
            )
        return jnp.concatenate(results, axis=0)

    count = batch * levels
    pieces = []
    for part in range(3):
        block = members[part].astype(F32) * field[part, :, :, :cells][None]
        edge = edges[part].astype(F32) * field[part, :, :, cells:][None]
        pieces.append(jnp.concatenate([block, edge], axis=-1).reshape(count * rows, 2 * cells))
    out[...] = scale * smooth(pieces, count).reshape(out.shape)

    @pl.when(pl.program_id(0) == 0)
    def _():
        pieces = [field[part].reshape(levels * rows, 2 * cells) for part in range(3)]
        static_out[...] = sigma[...] * smooth(pieces, levels).reshape(static_out.shape)


def shift(block, axis, step):
    count = lax.axis_size(axis)
    return lax.ppermute(block, axis, [(i, (i + step) % count) for i in range(count)])


def toeplitz(taps, shape, centre):
    offset = iota(shape, 0) - iota(shape, 1) + centre
    return jnp.sum(
        jnp.where(offset[:, :, None] == iota((1, 1, taps.shape[0]), 2), taps[None, None, :], 0.0),
        axis=2,
    )


def block_diagonal(matrix, count):
    rows, cols = matrix.shape
    tiled = jnp.tile(matrix, (count, count))
    return jnp.where(iota(tiled.shape, 0) // rows == iota(tiled.shape, 1) // cols, tiled, 0.0)


def divisor(count, limit):
    return max(n for n in range(1, count + 1) if count % n == 0 and (n <= limit or n == 1))


def per_device(
    ensemble,
    static_sigma,
    lat_taps,
    lon_taps,
    step_len,
    send_cols,
    send_count,
    obs_ref,
    obs_level,
    obs_weight,
    innovation,
    obs_precision,
):
    members, levels, rows, cells = ensemble.shape
    half = (lat_taps.shape[0] - 1) // 2
    n_lat, n_lon = lax.axis_size("lat"), lax.axis_size("lon")
    devices = n_lat * n_lon
    slots = send_cols.shape[3]
    both = ("lat", "lon")
    scale = HYBRID_ENSEMBLE / math.sqrt(members - 1)
    lat_at = lax.axis_index("lat")
    lon_at = lax.axis_index("lon")

    received = lax.all_to_all(send_count, both, split_axis=2, concat_axis=2, tiled=True).reshape(-1)
    ends = jnp.cumsum(received)
    starts = ends - received
    positions = obs_ref.reshape(obs_ref.shape[2], -1)
    past = positions[:, :, None] >= ends[None, None, :]
    source = jnp.sum(past.astype(jnp.int32), axis=2)
    lo = positions - jnp.sum(jnp.where(past, received[None, None, :], 0), axis=2)
    hi = source * levels + obs_level.reshape(1, -1)
    weight = obs_weight.reshape(positions.shape)
    innov = innovation.reshape(1, -1)
    prec = obs_precision.reshape(1, -1)

    groups = devices // levels
    per_group = members // groups
    device_at = lat_at * n_lon + lon_at
    level_at = device_at % levels
    spread = (
        ensemble.reshape(groups, per_group, levels, rows, cells)
        .transpose(0, 2, 1, 3, 4)
        .reshape(devices, per_group, rows, cells)
    )
    whole = lax.all_to_all(spread, both, split_axis=0, concat_axis=0, tiled=True)

    pick = jnp.concatenate(
        [
            (iota((half, cells), 1) == iota((half, cells), 0) + cells - half),
            (iota((half, cells), 1) == iota((half, cells), 0)),
        ],
        axis=0,
    ).astype(BF16)
    sides = lax.dot_general(
        pick,
        ensemble.reshape(-1, cells),
        (((1,), (1,)), ((), ())),
        preferred_element_type=BF16,
    )
    sides = jnp.concatenate([shift(sides[:half], "lon", 1), shift(sides[half:], "lon", -1)], axis=0)
    block3 = jnp.stack([shift(ensemble, "lat", 1), ensemble, shift(ensemble, "lat", -1)])
    sides3 = jnp.stack([shift(sides, "lat", 1), sides, shift(sides, "lat", -1)])
    place = (iota((2 * half, cells), 0) == iota((2 * half, cells), 1)).astype(BF16)
    edges3 = lax.dot_general(
        sides3, place, (((1,), (0,)), ((), ())), preferred_element_type=BF16
    ).reshape(block3.shape)

    whole_lat = toeplitz(lat_taps, (n_lat * rows, n_lat * rows), half).T
    lat_cov = jnp.dot(whole_lat, whole_lat.T, precision=lax.Precision.HIGHEST)
    lat_cov = block_diagonal(
        lat_cov, divisor(per_group + 1, max(1, 256 // (n_lat * rows)))
    )
    lon_corr = jnp.sum(
        jnp.where(
            iota((4 * half + 1, lon_taps.shape[0], lon_taps.shape[0]), 1)
            - iota((4 * half + 1, lon_taps.shape[0], lon_taps.shape[0]), 2)
            + 2 * half
            == iota((4 * half + 1, lon_taps.shape[0], lon_taps.shape[0]), 0),
            lon_taps[None, :, None] * lon_taps[None, None, :],
            0.0,
        ),
        axis=(1, 2),
    )
    lon_cov = toeplitz(lon_corr, (3 * cells, cells), 2 * half - cells)
    reverse = lon_taps[::-1]
    extended = toeplitz(reverse, (cells + 2 * half, cells), 0)
    lon_adjoint = jnp.concatenate(
        [
            extended[half : half + cells],
            extended[:half],
            extended[half + cells :],
            jnp.zeros((cells - 2 * half, cells), F32),
        ],
        axis=0,
    )
    lat_adjoint = block_diagonal(
        toeplitz(lat_taps[::-1], (rows + 2 * half, rows), 0).T, levels
    )

    wide_slots = max(slots, 256)
    cols = send_cols.reshape(-1, wide_slots)
    per_row = wide_slots // slots

    def to_buffer(packed):
        if per_row == 1:
            return packed
        return (
            packed.reshape(-1, levels, per_row, slots)
            .transpose(0, 2, 1, 3)
            .reshape(devices, levels, slots)
        )

    def from_buffer(buffer):
        if per_row == 1:
            return buffer
        return (
            buffer.reshape(-1, per_row, levels, slots)
            .transpose(0, 2, 1, 3)
            .reshape(-1, levels, wide_slots)
        )

    def route(buffer):
        return lax.all_to_all(buffer, both, split_axis=0, concat_axis=0, tiled=True)

    held = jnp.zeros((levels, rows, cells), F32)
    table = None
    for iteration in range(step_len.shape[0]):
        if iteration > 0:
            sent = jnp.broadcast_to(held[None], (groups,) + held.shape).reshape(
                devices, rows, cells
            )
            field = route(sent)
            static_coef = jnp.where(
                device_at < levels, HYBRID_STATIC**2 * static_sigma[level_at] ** 2, 0.0
            )
            coef = jnp.stack([static_coef, jnp.full((), scale * scale, F32)])
            height = n_lat * rows
            fields = per_group + 1
            part = pl.pallas_call(
                functools.partial(covariance_kernel, n_lat, n_lon),
                out_shape=jax.ShapeDtypeStruct((devices, rows, cells), F32),
                in_specs=[pl.BlockSpec(memory_space=pltpu.SMEM)] + [VMEM] * 4,
                out_specs=VMEM,
                scratch_shapes=[
                    pltpu.VMEM((fields * height, (n_lon + 2) * cells), F32),
                    pltpu.VMEM((fields * height, n_lon * cells), F32),
                ],
                name="covariance",
            )(coef, whole, field, lat_cov, lon_cov)
            increment = jnp.sum(
                route(part).reshape(groups, levels, rows, cells), axis=0
            )
            packed = pl.pallas_call(
                slots_kernel,
                out_shape=jax.ShapeDtypeStruct((cols.shape[0], levels, wide_slots), F32),
                in_specs=[VMEM, VMEM],
                out_specs=VMEM,
                name="to_slots",
            )(cols, increment.transpose(1, 0, 2).reshape(rows * levels, cells))
            table = route(to_buffer(packed)).reshape(devices * levels, slots)
        departure, pushed = observe(
            table, hi, lo, weight, innov, prec, devices * levels, slots
        )
        incoming = from_buffer(route(pushed.reshape(devices, levels, slots)))
        forcing = pl.pallas_call(
            columns_kernel,
            out_shape=jax.ShapeDtypeStruct((rows * levels, cells), F32),
            in_specs=[VMEM, VMEM],
            out_specs=VMEM,
            name="to_columns",
        )(cols, incoming)
        forcing = forcing.reshape(rows, levels, cells).transpose(1, 0, 2)
        held = held - step_len[iteration] * (forcing + held)

    low = shift(held[:, :, cells - half :], "lon", 1)
    high = shift(held[:, :, :half], "lon", -1)
    wide = jnp.concatenate(
        [held, low, high, jnp.zeros((levels, rows, cells - 2 * half), F32)], axis=2
    )
    above = jnp.where(lat_at > 0, shift(wide, "lat", 1), 0.0)
    below = jnp.where(lat_at < n_lat - 1, shift(wide, "lat", -1), 0.0)
    wide3 = jnp.stack([above, wide, below])
    batch = divisor(members, 8)
    sigma = jnp.broadcast_to(
        (HYBRID_STATIC * static_sigma)[:, None, None], (levels, rows, cells)
    )
    member_spec = pl.BlockSpec((3, batch, levels, rows, cells), lambda k: (0, k, 0, 0, 0))
    control, static = pl.pallas_call(
        functools.partial(adjoint_kernel, scale),
        grid=(members // batch,),
        out_shape=(
            jax.ShapeDtypeStruct(ensemble.shape, F32),
            jax.ShapeDtypeStruct((levels, rows, cells), F32),
        ),
        in_specs=[member_spec, member_spec] + [VMEM] * 4,
        out_specs=(
            pl.BlockSpec((batch, levels, rows, cells), lambda k: (k, 0, 0, 0)),
            pl.BlockSpec((levels, rows, cells), lambda k: (0, 0, 0)),
        ),
        name="adjoint",
    )(block3, edges3, wide3, sigma, lon_adjoint, lat_adjoint)
    return control, static, departure.reshape(1, 1, -1)


def solution(mesh):
    return jax.shard_map(
        per_device,
        mesh=mesh,
        in_specs=(
            P(None, None, "lat", "lon"),
            P(),
            P(),
            P(),
            P(),
            P("lat", "lon", None, None),
            P("lat", "lon", None),
            P("lat", "lon", None, None),
            P("lat", "lon", None),
            P("lat", "lon", None, None),
            P("lat", "lon", None),
            P("lat", "lon", None),
        ),
        out_specs=(P(None, None, "lat", "lon"), P(None, "lat", "lon"), P("lat", "lon", None)),
        check_vma=False,
    )
```

```python
import functools
import math

import jax
import jax.numpy as jnp
from jax import lax
from jax.experimental import pallas as pl
from jax.experimental.pallas import tpu as pltpu
from jax.sharding import PartitionSpec as P

HYBRID_STATIC = 0.5
HYBRID_ENSEMBLE = 0.8660254037844386
BF16 = jnp.bfloat16
F32 = jnp.float32
MESH = pl.DeviceIdType.MESH
VMEM = pl.BlockSpec(memory_space=pltpu.VMEM)


def halves(x):
    high = x.astype(BF16)
    return high, (x - high.astype(F32)).astype(BF16)


def dot(a, b):
    return jnp.dot(a, b, preferred_element_type=F32)


def dot_nt(a, b):
    return lax.dot_general(a, b, (((1,), (1,)), ((), ())), preferred_element_type=F32)


def dot3(a, b):
    a_high, a_low = halves(a)
    b_high, b_low = halves(b)
    return dot(a_high, b_high) + dot(a_high, b_low) + dot(a_low, b_high)


def iota(shape, dim):
    return lax.broadcasted_iota(jnp.int32, shape, dim)


def obs_step(table, hi, lo, weight, innov, prec, departure, out, rows, slots):
    chunk = 512 if rows <= 256 else 256
    points = hi.shape[0]
    if table is not None:
        table_high, table_low = halves(table[...].reshape(rows, slots))

    def step(index, carry):
        where = pl.ds(pl.multiple_of(index * chunk, chunk), chunk)
        row_ids = iota((rows, chunk), 0)
        slot_ids = iota((slots, chunk), 0)
        value = -innov[:, where]
        if table is not None:
            for q in range(points):
                lo_hot = jnp.where(slot_ids == lo[q : q + 1, where], 1.0, 0.0).astype(BF16)
                product = dot(table_high, lo_hot) + dot(table_low, lo_hot)
                picked = jnp.sum(
                    jnp.where(row_ids == hi[q : q + 1, where], product, 0.0), axis=0, keepdims=True
                )
                value = value + weight[q : q + 1, where] * picked
            departure[:, where] = value
        value = prec[:, where] * value
        total = None
        for q in range(points):
            lo_hot = jnp.where(slot_ids == lo[q : q + 1, where], 1.0, 0.0).astype(BF16)
            pushed = weight[q : q + 1, where] * value
            high = pushed.astype(BF16).astype(F32)
            chosen = row_ids == hi[q : q + 1, where]
            term = dot_nt(jnp.where(chosen, high, 0.0).astype(BF16), lo_hot) + dot_nt(
                jnp.where(chosen, pushed - high, 0.0).astype(BF16), lo_hot
            )
            total = term if total is None else total + term
        return carry + total

    total = lax.fori_loop(0, hi.shape[1] // chunk, step, jnp.zeros((rows, slots), F32))
    out[...] = total.reshape(out.shape)


def to_slots(cols, field, out):
    levels, lat_rows, cells = field.shape
    slots = out.shape[2]
    width = cols.shape[1]
    per_row = width // slots
    rows = jnp.concatenate([field[:, r, :] for r in range(lat_rows)], axis=0)
    count = rows.shape[0]
    both = jnp.concatenate(halves(rows), axis=0)

    def step(index, carry):
        col = cols[pl.ds(index, 1), :]
        cell_hot = jnp.where(iota((cells, width), 0) == col % cells, 1.0, 0.0).astype(BF16)
        product = dot(both, cell_hot)
        product = product[:count] + product[count:]
        row = jnp.broadcast_to(col // cells, (levels, width))
        total = jnp.zeros((levels, width), F32)
        for r in range(lat_rows):
            total = jnp.where(row == r, product[r * levels : (r + 1) * levels], total)
        for j in range(per_row):
            out[index * per_row + j] = total[:, j * slots : (j + 1) * slots]
        return carry

    lax.fori_loop(0, cols.shape[0], step, 0)


def to_columns(cols, values, shape):
    levels, lat_rows, cells = shape
    slots = values.shape[2]
    width = cols.shape[1]
    per_row = width // slots
    count = levels * lat_rows

    def step(index, total):
        col = cols[pl.ds(index, 1), :]
        cell_hot = jnp.where(iota((cells, width), 0) == col % cells, 1.0, 0.0).astype(BF16)
        chosen = iota((lat_rows, width), 0) == col // cells
        value = values[index * per_row]
        if per_row > 1:
            value = jnp.concatenate(
                [values[index * per_row + j] for j in range(per_row)], axis=1
            )
        high = value.astype(BF16).astype(F32)
        low = value - high
        parts = [jnp.where(chosen, high[l : l + 1], 0.0) for l in range(levels)]
        parts += [jnp.where(chosen, low[l : l + 1], 0.0) for l in range(levels)]
        return total + dot_nt(jnp.concatenate(parts, axis=0).astype(BF16), cell_hot)

    total = lax.fori_loop(0, cols.shape[0], step, jnp.zeros((2 * count, cells), F32))
    return (total[:count] + total[count:]).reshape(shape)


def covariance(blocks_lat, blocks_lon, coef, members, forcing, lat_op, lon_op, out, wide, mid):
    count = members.shape[1]
    rows, cells = forcing.shape[1:]
    height = blocks_lat * rows
    fields = count + 1
    for b in range(blocks_lon):
        for a in range(blocks_lat):
            spot = a * blocks_lon + b
            part = forcing[spot]
            for k in range(fields):
                piece = part if k == count else members[spot, k].astype(F32) * part
                at = pl.ds(k * height + a * rows, rows)
                wide[at, (b + 1) * cells : (b + 2) * cells] = piece
                if b == 0:
                    wide[at, (blocks_lon + 1) * cells :] = piece
                if b == blocks_lon - 1:
                    wide[at, :cells] = piece
    lon_high, lon_low = halves(lon_op[...])
    for b in range(blocks_lon):
        high, low = halves(wide[:, b * cells : (b + 3) * cells])
        mid[:, b * cells : (b + 1) * cells] = (
            dot(high, lon_high) + dot(high, lon_low) + dot(low, lon_high)
        )
    size = lat_op.shape[0]
    group = size // height
    for first in range(0, fields, group):
        where = pl.ds(first * height, size)
        wide[where, : blocks_lon * cells] = dot3(lat_op[...], mid[where, :])
    for a in range(blocks_lat):
        for b in range(blocks_lon):
            spot = a * blocks_lon + b
            total = coef[0] * wide[
                pl.ds(count * height + a * rows, rows), b * cells : (b + 1) * cells
            ]
            for k in range(count):
                total = total + coef[1] * (
                    members[spot, k].astype(F32)
                    * wide[pl.ds(k * height + a * rows, rows), b * cells : (b + 1) * cells]
                )
            out[spot] = total


def main_kernel(
    n_lat, n_lon, iterations,
    coef, step, ens, sides, count_row, cols, pos, level, weight, innov, prec, lat_op, lon_op,
    departure, near, near_sides, near_held,
    counts, whole, pushed, incoming, field, part, part_in, packed, table, held, wide, mid, hi, lo,
    ex_send, ex_recv, near_send, near_recv, side_send, side_recv, held_send, held_recv,
):
    lat_at, lon_at = lax.axis_index("lat"), lax.axis_index("lon")
    me = lat_at * n_lon + lon_at
    devices = n_lat * n_lon
    levels, rows, cells = held.shape
    slots = pushed.shape[2]
    per_group = whole.shape[1]
    half = sides.shape[0] // 2

    def place(d):
        return (d // n_lon, d % n_lon)

    barrier = pltpu.get_barrier_semaphore()

    def greet(k, carry):
        pl.semaphore_signal(
            barrier, inc=1, device_id=place((me + k) % devices), device_id_type=MESH
        )
        return carry

    lax.fori_loop(1, devices, greet, 0)
    pl.semaphore_wait(barrier, devices - 1)

    def send(source, target, number, first=1, last=None):
        def one(k, carry):
            d = (me + k) % devices
            pltpu.make_async_remote_copy(
                src_ref=source(d),
                dst_ref=target.at[me],
                send_sem=ex_send.at[number],
                recv_sem=ex_recv.at[number],
                device_id=place(d),
                device_id_type=MESH,
            ).start()
            return carry

        lax.fori_loop(first, devices if last is None else last, one, 0)

    def wait(target, number):
        every = target.at[pl.ds(0, devices - 1)]
        copy = pltpu.make_async_remote_copy(
            src_ref=every,
            dst_ref=every,
            send_sem=ex_send.at[number],
            recv_sem=ex_recv.at[number],
            device_id=place((me + 1) % devices),
            device_id_type=MESH,
        )
        copy.wait_send()
        copy.wait_recv()

    def members_of(d):
        return ens.at[pl.ds((d // levels) * per_group, per_group), d % levels]

    send(lambda d: count_row, counts, 0)
    early = max(2, devices // 4)
    send(members_of, whole, 1, 1, early)
    counts[me] = count_row[...]
    whole[me] = ens[pl.ds((me // levels) * per_group, per_group), me % levels]
    wait(counts, 0)
    received = jnp.concatenate([counts[d] for d in range(devices)], axis=0)
    width = received.shape[1]
    column = jnp.sum(
        jnp.where(iota((devices, width), 1) == me, received, 0), axis=1, keepdims=True
    )
    as_row = jnp.sum(
        jnp.where(iota((devices, width), 0) == iota((devices, width), 1), column, 0),
        axis=0, keepdims=True,
    )
    ends = jnp.sum(
        jnp.where(iota((devices, width), 1) <= iota((devices, width), 0), as_row, 0),
        axis=1, keepdims=True,
    )
    for q in range(pos.shape[0]):
        place_q = pos[q : q + 1, :]
        past = place_q >= ends
        source = jnp.sum(jnp.where(past, 1, 0), axis=0, keepdims=True)
        lo[q : q + 1, :] = place_q - jnp.sum(jnp.where(past, column, 0), axis=0, keepdims=True)
        hi[q : q + 1, :] = source * levels + level[...]

    number = 2
    for iteration in range(iterations):
        before = iteration - 1
        if iteration > 0:
            send(lambda d: held.at[d % levels], field.at[before], number)
            field[before, me] = held[me % levels]
            if iteration == 1:
                wait(whole, 1)
            wait(field.at[before], number)
            if iteration == 1:
                near_copies(
                    n_lat, n_lon, lat_at, lon_at, half, ens, sides, near, near_sides,
                    near_send, near_recv, side_send, side_recv, True,
                )
            covariance(
                n_lat, n_lon, coef, whole, field.at[before], lat_op, lon_op, part, wide, mid
            )
            send(lambda d: part.at[d], part_in.at[before], number + 1)
            part_in[before, me] = part[me]
            wait(part_in.at[before], number + 1)
            total = part_in[before, 0:levels]
            for g in range(1, devices // levels):
                total = total + part_in[before, g * levels : (g + 1) * levels]
            part[0:levels] = total
            to_slots(cols, part.at[0:levels], packed)
            send(lambda d: packed.at[d], table.at[before], number + 2)
            table[before, me] = packed[me]
            wait(table.at[before], number + 2)
            number += 3
        obs_step(
            table.at[before] if iteration > 0 else None,
            hi, lo, weight, innov, prec, departure, pushed, devices * levels, slots,
        )
        send(lambda d: pushed.at[d], incoming.at[iteration], number)
        if iteration == 0:
            send(members_of, whole, 1, early)
        incoming[iteration, me] = pushed[me]
        wait(incoming.at[iteration], number)
        number += 1
        forcing = to_columns(cols, incoming.at[iteration], held.shape)
        if iteration == 0:
            held[...] = -step[0] * forcing
        else:
            held[...] = held[...] - step[iteration] * (forcing + held[...])

    held_copies(n_lat, n_lon, lat_at, lon_at, held, near_held, held_send, held_recv, True)
    near_held[1, 1] = held[...]
    near_copies(
        n_lat, n_lon, lat_at, lon_at, half, ens, sides, near, near_sides,
        near_send, near_recv, side_send, side_recv, False,
    )
    held_copies(n_lat, n_lon, lat_at, lon_at, held, near_held, held_send, held_recv, False)


def exchange_pair(begin, has_send, has_recv, **copy):
    made = pltpu.make_async_remote_copy(device_id_type=MESH, **copy)
    if begin:
        pl.when(has_send)(made.start)
    else:
        pl.when(has_send)(made.wait_send)
        pl.when(has_recv)(made.wait_recv)


def lat_has(n_lat, lat_at, step):
    send = jnp.logical_and(lat_at + step >= 0, lat_at + step < n_lat)
    recv = jnp.logical_and(lat_at - step >= 0, lat_at - step < n_lat)
    return send, recv


def near_copies(
    n_lat, n_lon, lat_at, lon_at, half, ens, sides, near, near_sides,
    near_send, near_recv, side_send, side_recv, begin,
):
    for index, step in enumerate((1, -1)):
        has = lat_has(n_lat, lat_at, step)
        exchange_pair(
            begin, *has,
            src_ref=ens, dst_ref=near.at[index],
            send_sem=near_send.at[index], recv_sem=near_recv.at[index],
            device_id=((lat_at + step + n_lat) % n_lat, lon_at),
        )
    for up, step in enumerate((1, 0, -1)):
        has = lat_has(n_lat, lat_at, step)
        for side, turn in enumerate((1, -1)):
            exchange_pair(
                begin, *has,
                src_ref=sides.at[pl.ds(side * half, half)],
                dst_ref=near_sides.at[up, pl.ds(side * half, half)],
                send_sem=side_send.at[up * 2 + side], recv_sem=side_recv.at[up * 2 + side],
                device_id=((lat_at + step + n_lat) % n_lat, (lon_at + turn + n_lon) % n_lon),
            )


def held_copies(n_lat, n_lon, lat_at, lon_at, held, near_held, held_send, held_recv, begin):
    for up, step in enumerate((1, 0, -1)):
        has = lat_has(n_lat, lat_at, step)
        for side, turn in enumerate((1, 0, -1)):
            if step == 0 and turn == 0:
                continue
            exchange_pair(
                begin, *has,
                src_ref=held, dst_ref=near_held.at[up, side],
                send_sem=held_send.at[up * 3 + side], recv_sem=held_recv.at[up * 3 + side],
                device_id=((lat_at + step + n_lat) % n_lat, (lon_at + turn + n_lon) % n_lon),
            )


def adjoint_kernel(scale, keep, members, near, edges, field, sigma, lon_op, lat_op, out, static_out):
    batch, levels, rows, cells = out.shape
    lon_high, lon_low = halves(lon_op[...])

    def smooth(pieces, count):
        passes = []
        for piece in pieces:
            high, low = halves(piece)
            passes.append(
                (dot(high, lon_high) + dot(high, lon_low) + dot(low, lon_high)).reshape(
                    count, rows, cells
                )
            )
        stacked = jnp.concatenate(passes, axis=1)
        group = lat_op.shape[0] // rows
        results = []
        for first in range(0, count, group):
            results.append(
                dot3(
                    lat_op[...],
                    stacked[first : first + group].reshape(group * 3 * rows, cells),
                )
            )
        return jnp.concatenate(results, axis=0)

    count = batch * levels
    pieces = []
    for part in range(3):
        values = members[...] if part == 1 else near[part // 2]
        block = values.astype(F32) * field[part, :, :, :cells][None]
        edge = edges[part].astype(F32) * field[part, :, :, cells:][None]
        piece = jnp.concatenate([block, edge], axis=-1).reshape(count * rows, 2 * cells)
        pieces.append(piece if part == 1 else jnp.where(keep[part // 2] > 0, piece, 0.0))
    out[...] = scale * smooth(pieces, count).reshape(out.shape)

    @pl.when(pl.program_id(0) == 0)
    def _():
        pieces = [field[part].reshape(levels * rows, 2 * cells) for part in range(3)]
        static_out[...] = sigma[...] * smooth(pieces, levels).reshape(static_out.shape)


def shift(block, axis, step):
    count = lax.axis_size(axis)
    return lax.ppermute(block, axis, [(i, (i + step) % count) for i in range(count)])


def toeplitz(taps, shape, centre):
    offset = iota(shape, 0) - iota(shape, 1) + centre
    return jnp.sum(
        jnp.where(offset[:, :, None] == iota((1, 1, taps.shape[0]), 2), taps[None, None, :], 0.0),
        axis=2,
    )


def block_diagonal(matrix, count):
    rows, cols = matrix.shape
    tiled = jnp.tile(matrix, (count, count))
    return jnp.where(iota(tiled.shape, 0) // rows == iota(tiled.shape, 1) // cols, tiled, 0.0)


def divisor(count, limit):
    return max(n for n in range(1, count + 1) if count % n == 0 and (n <= limit or n == 1))


def per_device(
    ensemble,
    static_sigma,
    lat_taps,
    lon_taps,
    step_len,
    send_cols,
    send_count,
    obs_ref,
    obs_level,
    obs_weight,
    innovation,
    obs_precision,
):
    members, levels, rows, cells = ensemble.shape
    half = (lat_taps.shape[0] - 1) // 2
    n_lat, n_lon = lax.axis_size("lat"), lax.axis_size("lon")
    devices = n_lat * n_lon
    slots = send_cols.shape[3]
    scale = HYBRID_ENSEMBLE / math.sqrt(members - 1)
    lat_at = lax.axis_index("lat")
    lon_at = lax.axis_index("lon")

    positions = obs_ref.reshape(obs_ref.shape[2], -1)
    weight = obs_weight.reshape(positions.shape)
    groups = devices // levels
    per_group = members // groups
    device_at = lat_at * n_lon + lon_at
    level_at = device_at % levels

    pick = jnp.concatenate(
        [
            (iota((half, cells), 1) == iota((half, cells), 0) + cells - half),
            (iota((half, cells), 1) == iota((half, cells), 0)),
        ],
        axis=0,
    ).astype(BF16)
    sides = lax.dot_general(
        pick,
        ensemble.reshape(-1, cells),
        (((1,), (1,)), ((), ())),
        preferred_element_type=BF16,
    )

    whole_lat = toeplitz(lat_taps, (n_lat * rows, n_lat * rows), half).T
    lat_cov = jnp.dot(whole_lat, whole_lat.T, precision=lax.Precision.HIGHEST)
    lat_cov = block_diagonal(
        lat_cov, divisor(per_group + 1, max(1, 256 // (n_lat * rows)))
    )
    lon_corr = jnp.sum(
        jnp.where(
            iota((4 * half + 1, lon_taps.shape[0], lon_taps.shape[0]), 1)
            - iota((4 * half + 1, lon_taps.shape[0], lon_taps.shape[0]), 2)
            + 2 * half
            == iota((4 * half + 1, lon_taps.shape[0], lon_taps.shape[0]), 0),
            lon_taps[None, :, None] * lon_taps[None, None, :],
            0.0,
        ),
        axis=(1, 2),
    )
    lon_cov = toeplitz(lon_corr, (3 * cells, cells), 2 * half - cells)
    reverse = lon_taps[::-1]
    extended = toeplitz(reverse, (cells + 2 * half, cells), 0)
    lon_adjoint = jnp.concatenate(
        [
            extended[half : half + cells],
            extended[:half],
            extended[half + cells :],
            jnp.zeros((cells - 2 * half, cells), F32),
        ],
        axis=0,
    )
    lat_adjoint = block_diagonal(
        toeplitz(lat_taps[::-1], (rows + 2 * half, rows), 0).T, levels
    )

    wide_slots = max(slots, 256)
    cols = send_cols.reshape(-1, wide_slots)
    iterations = step_len.shape[0]
    later = max(1, iterations - 1)
    fields = per_group + 1
    height = n_lat * rows
    static_coef = jnp.where(
        device_at < levels, HYBRID_STATIC**2 * static_sigma[level_at] ** 2, 0.0
    )
    coef = jnp.stack([static_coef, jnp.full((), scale * scale, F32)])
    count_width = -(-devices // 128) * 128
    count_row = jnp.pad(send_count.reshape(1, -1), ((0, 0), (0, count_width - devices)))
    smem = pl.BlockSpec(memory_space=pltpu.SMEM)
    hbm = pl.BlockSpec(memory_space=pl.ANY)
    exchanges = 2 + iterations + 3 * (iterations - 1)
    departure, near, near_sides, near_held = pl.pallas_call(
        functools.partial(main_kernel, n_lat, n_lon, iterations),
        out_shape=(
            jax.ShapeDtypeStruct((1, positions.shape[1]), F32),
            jax.ShapeDtypeStruct((2,) + ensemble.shape, BF16),
            jax.ShapeDtypeStruct((3,) + sides.shape, BF16),
            jax.ShapeDtypeStruct((3, 3, levels, rows, cells), F32),
        ),
        in_specs=[smem] * 2 + [VMEM] * 11,
        out_specs=(VMEM, hbm, VMEM, VMEM),
        scratch_shapes=[
            pltpu.VMEM((devices, 1, count_width), jnp.int32),
            pltpu.VMEM((devices, per_group, rows, cells), BF16),
            pltpu.VMEM((devices, levels, slots), F32),
            pltpu.VMEM((iterations, devices, levels, slots), F32),
            pltpu.VMEM((later, devices, rows, cells), F32),
            pltpu.VMEM((devices, rows, cells), F32),
            pltpu.VMEM((later, devices, rows, cells), F32),
            pltpu.VMEM((devices, levels, slots), F32),
            pltpu.VMEM((later, devices, levels, slots), F32),
            pltpu.VMEM((levels, rows, cells), F32),
            pltpu.VMEM((fields * height, (n_lon + 2) * cells), F32),
            pltpu.VMEM((fields * height, n_lon * cells), F32),
            pltpu.VMEM(positions.shape, jnp.int32),
            pltpu.VMEM(positions.shape, jnp.int32),
            pltpu.SemaphoreType.DMA((exchanges,)),
            pltpu.SemaphoreType.DMA((exchanges,)),
            pltpu.SemaphoreType.DMA((2,)),
            pltpu.SemaphoreType.DMA((2,)),
            pltpu.SemaphoreType.DMA((6,)),
            pltpu.SemaphoreType.DMA((6,)),
            pltpu.SemaphoreType.DMA((9,)),
            pltpu.SemaphoreType.DMA((9,)),
        ],
        compiler_params=pltpu.CompilerParams(collective_id=0, has_side_effects=True),
        name="analysis",
    )(
        coef, step_len, ensemble, sides, count_row, cols, positions,
        obs_level.reshape(1, -1), weight, innovation.reshape(1, -1),
        obs_precision.reshape(1, -1), lat_cov, lon_cov,
    )
    wide3 = jnp.concatenate(
        [
            near_held[:, 1],
            near_held[:, 0, :, :, cells - half :],
            near_held[:, 2, :, :, :half],
            jnp.zeros((3, levels, rows, cells - 2 * half), F32),
        ],
        axis=3,
    )
    keep = jnp.stack([lat_at > 0, lat_at < n_lat - 1]).astype(jnp.int32)
    wide3 = jnp.where(
        jnp.stack([keep[0], jnp.ones((), jnp.int32), keep[1]])[:, None, None, None] > 0, wide3, 0.0
    )
    sides_id = (iota((2 * half, cells), 0) == iota((2 * half, cells), 1)).astype(BF16)
    edges3 = lax.dot_general(
        near_sides, sides_id, (((1,), (0,)), ((), ())), preferred_element_type=BF16
    ).reshape((3,) + ensemble.shape)
    batch = divisor(members, 8)
    sigma = jnp.broadcast_to(
        (HYBRID_STATIC * static_sigma)[:, None, None], (levels, rows, cells)
    )
    own_spec = pl.BlockSpec((batch, levels, rows, cells), lambda k: (k, 0, 0, 0))
    near_spec = pl.BlockSpec((2, batch, levels, rows, cells), lambda k: (0, k, 0, 0, 0))
    edge_spec = pl.BlockSpec((3, batch, levels, rows, cells), lambda k: (0, k, 0, 0, 0))
    control, static = pl.pallas_call(
        functools.partial(adjoint_kernel, scale),
        grid=(members // batch,),
        out_shape=(
            jax.ShapeDtypeStruct(ensemble.shape, F32),
            jax.ShapeDtypeStruct((levels, rows, cells), F32),
        ),
        in_specs=[smem, own_spec, near_spec, edge_spec] + [VMEM] * 4,
        out_specs=(
            pl.BlockSpec((batch, levels, rows, cells), lambda k: (k, 0, 0, 0)),
            pl.BlockSpec((levels, rows, cells), lambda k: (0, 0, 0)),
        ),
        name="adjoint",
    )(keep, ensemble, near, edges3, wide3, sigma, lon_adjoint, lat_adjoint)
    return control, static, departure.reshape(1, 1, -1)


def solution(mesh):
    return jax.shard_map(
        per_device,
        mesh=mesh,
        in_specs=(
            P(None, None, "lat", "lon"),
            P(),
            P(),
            P(),
            P(),
            P("lat", "lon", None, None),
            P("lat", "lon", None),
            P("lat", "lon", None, None),
            P("lat", "lon", None),
            P("lat", "lon", None, None),
            P("lat", "lon", None),
            P("lat", "lon", None),
        ),
        out_specs=(P(None, None, "lat", "lon"), P(None, "lat", "lon"), P("lat", "lon", None)),
        check_vma=False,
    )
```

```python
import functools
import math

import jax
import jax.numpy as jnp
from jax import lax
from jax.experimental import pallas as pl
from jax.experimental.pallas import tpu as pltpu
from jax.sharding import PartitionSpec as P

HYBRID_STATIC = 0.5
HYBRID_ENSEMBLE = 0.8660254037844386
BF16 = jnp.bfloat16
F32 = jnp.float32
MESH = pl.DeviceIdType.MESH
CHUNKS = 4
VMEM = pl.BlockSpec(memory_space=pltpu.VMEM)


def halves(x):
    high = x.astype(BF16)
    return high, (x - high.astype(F32)).astype(BF16)


def dot(a, b):
    return jnp.dot(a, b, preferred_element_type=F32)


def dot_nt(a, b):
    return lax.dot_general(a, b, (((1,), (1,)), ((), ())), preferred_element_type=F32)


def dot3(a, b):
    a_high, a_low = halves(a)
    b_high, b_low = halves(b)
    return dot(a_high, b_high) + dot(a_high, b_low) + dot(a_low, b_high)


def iota(shape, dim):
    return lax.broadcasted_iota(jnp.int32, shape, dim)


def obs_step(table, hi, lo, weight, innov, prec, departure, out, rows, slots):
    chunk = 512 if rows <= 256 else 256
    points = hi.shape[0]
    if table is not None:
        table_high, table_low = halves(table[...].reshape(rows, slots))

    def step(index, carry):
        where = pl.ds(pl.multiple_of(index * chunk, chunk), chunk)
        row_ids = iota((rows, chunk), 0)
        slot_ids = iota((slots, chunk), 0)
        value = -innov[:, where]
        if table is not None:
            for q in range(points):
                lo_hot = jnp.where(slot_ids == lo[q : q + 1, where], 1.0, 0.0).astype(BF16)
                product = dot(table_high, lo_hot) + dot(table_low, lo_hot)
                picked = jnp.sum(
                    jnp.where(row_ids == hi[q : q + 1, where], product, 0.0), axis=0, keepdims=True
                )
                value = value + weight[q : q + 1, where] * picked
            departure[:, where] = value
        value = prec[:, where] * value
        total = None
        for q in range(points):
            lo_hot = jnp.where(slot_ids == lo[q : q + 1, where], 1.0, 0.0).astype(BF16)
            pushed = weight[q : q + 1, where] * value
            high = pushed.astype(BF16).astype(F32)
            chosen = row_ids == hi[q : q + 1, where]
            term = dot_nt(jnp.where(chosen, high, 0.0).astype(BF16), lo_hot) + dot_nt(
                jnp.where(chosen, pushed - high, 0.0).astype(BF16), lo_hot
            )
            total = term if total is None else total + term
        return carry + total

    total = lax.fori_loop(0, hi.shape[1] // chunk, step, jnp.zeros((rows, slots), F32))
    out[...] = total.reshape(out.shape)


def cell_and_row(col, cells):
    if cells & (cells - 1):
        return col % cells, col // cells
    return jnp.bitwise_and(col, cells - 1), jnp.right_shift(col, cells.bit_length() - 1)


def to_slots(cols, field, out):
    levels, lat_rows, cells = field.shape
    slots = out.shape[2]
    width = cols.shape[1]
    per_row = width // slots
    rows = jnp.concatenate([field[:, r, :] for r in range(lat_rows)], axis=0)
    count = rows.shape[0]
    both = jnp.concatenate(halves(rows), axis=0)

    def step(index, carry):
        col = cols[pl.ds(index, 1), :]
        cell, at_row = cell_and_row(col, cells)
        cell_hot = jnp.where(iota((cells, width), 0) == cell, 1.0, 0.0).astype(BF16)
        product = dot(both, cell_hot)
        product = product[:count] + product[count:]
        row = jnp.broadcast_to(at_row, (levels, width))
        total = jnp.zeros((levels, width), F32)
        for r in range(lat_rows):
            total = jnp.where(row == r, product[r * levels : (r + 1) * levels], total)
        for j in range(per_row):
            out[index * per_row + j] = total[:, j * slots : (j + 1) * slots]
        return carry

    lax.fori_loop(0, cols.shape[0], step, 0, unroll=4)


def to_columns(cols, values, shape):
    levels, lat_rows, cells = shape
    slots = values.shape[2]
    width = cols.shape[1]
    per_row = width // slots
    count = levels * lat_rows

    def step(index, total):
        col = cols[pl.ds(index, 1), :]
        cell, at_row = cell_and_row(col, cells)
        cell_hot = jnp.where(iota((cells, width), 0) == cell, 1.0, 0.0).astype(BF16)
        chosen = iota((lat_rows, width), 0) == at_row
        value = values[index * per_row]
        if per_row > 1:
            value = jnp.concatenate(
                [values[index * per_row + j] for j in range(per_row)], axis=1
            )
        high = value.astype(BF16).astype(F32)
        low = value - high
        parts = [jnp.where(chosen, high[l : l + 1], 0.0) for l in range(levels)]
        parts += [jnp.where(chosen, low[l : l + 1], 0.0) for l in range(levels)]
        return total + dot_nt(jnp.concatenate(parts, axis=0).astype(BF16), cell_hot)

    total = lax.fori_loop(
        0, cols.shape[0], step, jnp.zeros((2 * count, cells), F32), unroll=4
    )
    return (total[:count] + total[count:]).reshape(shape)


def covariance(blocks_lat, blocks_lon, coef, members, forcing, lat_op, lon_op, out, wide, mid):
    count = members.shape[1]
    rows, cells = forcing.shape[1:]
    height = blocks_lat * rows
    fields = count + 1
    for b in range(blocks_lon):
        for a in range(blocks_lat):
            spot = a * blocks_lon + b
            part = forcing[spot]
            for k in range(fields):
                piece = part if k == count else members[spot, k].astype(F32) * part
                at = pl.ds(k * height + a * rows, rows)
                wide[at, (b + 1) * cells : (b + 2) * cells] = piece
                if b == 0:
                    wide[at, (blocks_lon + 1) * cells :] = piece
                if b == blocks_lon - 1:
                    wide[at, :cells] = piece
    lon_high, lon_low = halves(lon_op[...])
    for b in range(blocks_lon):
        high, low = halves(wide[:, b * cells : (b + 3) * cells])
        mid[:, b * cells : (b + 1) * cells] = (
            dot(high, lon_high) + dot(high, lon_low) + dot(low, lon_high)
        )
    size = lat_op.shape[0]
    group = size // height
    for first in range(0, fields, group):
        where = pl.ds(first * height, size)
        wide[where, : blocks_lon * cells] = dot3(lat_op[...], mid[where, :])
    for a in range(blocks_lat):
        for b in range(blocks_lon):
            spot = a * blocks_lon + b
            total = coef[0] * wide[
                pl.ds(count * height + a * rows, rows), b * cells : (b + 1) * cells
            ]
            for k in range(count):
                total = total + coef[1] * (
                    members[spot, k].astype(F32)
                    * wide[pl.ds(k * height + a * rows, rows), b * cells : (b + 1) * cells]
                )
            out[spot] = total


def banded(taps, offset):
    total = jnp.zeros(offset.shape, F32)
    for t in range(len(taps)):
        total = jnp.where(offset == t, taps[t], total)
    return total


def block_of(ids, size, count):
    total = jnp.zeros(ids.shape, jnp.int32)
    for b in range(1, count):
        total = total + jnp.where(ids >= b * size, 1, 0)
    return total


def make_operators(
    height, rows, cells, lat_taps, lon_taps, lat_op, lon_op, lat_adjoint, lon_adjoint
):
    count = lat_taps.shape[0]
    half = (count - 1) // 2
    lat = [lat_taps[t] for t in range(count)]
    lon = [lon_taps[t] for t in range(count)]
    shape = lat_op.shape
    blocks = shape[0] // height
    row, col = iota(shape, 0), iota(shape, 1)
    same = block_of(row, height, blocks) == block_of(col, height, blocks)
    high, low = halves(jnp.where(same, banded(lat, col - row + half), 0.0))
    lat_op[...] = dot_nt(high, high) + dot_nt(high, low) + dot_nt(low, high)
    corr = []
    for lag in range(-2 * half, 2 * half + 1):
        terms = [lon[t] * lon[t - lag] for t in range(count) if 0 <= t - lag < count]
        corr.append(functools.reduce(lambda a, b: a + b, terms))
    shape = lon_op.shape
    lon_op[...] = banded(corr, iota(shape, 0) - iota(shape, 1) + 2 * half - cells)
    shape = lon_adjoint.shape
    row = iota(shape, 0)
    spot = jnp.where(
        row < cells,
        row + half,
        jnp.where(
            row < cells + half, row - cells, jnp.where(row < cells + 2 * half, row, 4 * cells)
        ),
    )
    lon_adjoint[...] = banded(lon[::-1], spot - iota(shape, 1))
    shape = lat_adjoint.shape
    blocks = shape[0] // rows
    row, col = iota(shape, 0), iota(shape, 1)
    row_block, col_block = block_of(row, rows, blocks), block_of(col, 3 * rows, blocks)
    offset = (col - 3 * rows * col_block) - (row - rows * row_block)
    lat_adjoint[...] = jnp.where(row_block == col_block, banded(lat[::-1], offset), 0.0)


def make_sides(ens, sides):
    cells = ens.shape[3]
    half = sides.shape[0] // 2
    row, col = iota((2 * half, cells), 0), iota((2 * half, cells), 1)
    pick = jnp.where(col == jnp.where(row < half, row + cells - half, row - half), 1.0, 0.0)
    members = 8 if ens.shape[0] % 8 == 0 else 1
    size = members * ens.shape[1] * ens.shape[2]
    for first in range(0, ens.shape[0], members):
        some = ens[first : first + members].reshape(size, cells)
        at = first // members * size
        sides[:, at : at + size] = dot_nt(pick.astype(BF16), some).astype(BF16)


def main_kernel(
    n_lat, n_lon, iterations,
    coef, step, lat_taps, lon_taps, ens, count_row, cols, pos, level, weight, innov, prec,
    departure, near, near_sides, near_held, lat_adjoint, lon_adjoint,
    counts, whole, pushed, incoming, field, part, part_in, packed, table, held, wide, mid, hi, lo,
    sides, lat_op, lon_op,
    ex_send, ex_recv, near_send, near_recv, side_send, side_recv, held_send, held_recv,
):
    lat_at, lon_at = lax.axis_index("lat"), lax.axis_index("lon")
    me = lat_at * n_lon + lon_at
    devices = n_lat * n_lon
    levels, rows, cells = held.shape
    slots = pushed.shape[2]
    per_group = whole.shape[1]
    half = sides.shape[0] // 2

    def place(d):
        return (d // n_lon, d % n_lon)

    barrier = pltpu.get_barrier_semaphore()

    def greet(k, carry):
        pl.semaphore_signal(
            barrier, inc=1, device_id=place((me + k) % devices), device_id_type=MESH
        )
        return carry

    lax.fori_loop(1, devices, greet, 0)
    pl.semaphore_wait(barrier, devices - 1)

    def send(source, target, number, first=1, last=None):
        def one(k, carry):
            d = (me + k) % devices
            pltpu.make_async_remote_copy(
                src_ref=source(d),
                dst_ref=target.at[me],
                send_sem=ex_send.at[number],
                recv_sem=ex_recv.at[number],
                device_id=place(d),
                device_id_type=MESH,
            ).start()
            return carry

        lax.fori_loop(first, devices if last is None else last, one, 0)

    def wait(target, number):
        every = target.at[pl.ds(0, devices - 1)]
        copy = pltpu.make_async_remote_copy(
            src_ref=every,
            dst_ref=every,
            send_sem=ex_send.at[number],
            recv_sem=ex_recv.at[number],
            device_id=place((me + 1) % devices),
            device_id_type=MESH,
        )
        copy.wait_send()
        copy.wait_recv()

    def members_of(d):
        return ens.at[pl.ds((d // levels) * per_group, per_group), d % levels]

    send(lambda d: count_row, counts, 0)
    early = max(2, devices // 4)
    send(members_of, whole, 1, 1, early)
    counts[me] = count_row[...]
    whole[me] = ens[pl.ds((me // levels) * per_group, per_group), me % levels]
    wait(counts, 0)
    received = jnp.concatenate([counts[d] for d in range(devices)], axis=0)
    width = received.shape[1]
    column = jnp.sum(
        jnp.where(iota((devices, width), 1) == me, received, 0), axis=1, keepdims=True
    )
    as_row = jnp.sum(
        jnp.where(iota((devices, width), 0) == iota((devices, width), 1), column, 0),
        axis=0, keepdims=True,
    )
    ends = jnp.sum(
        jnp.where(iota((devices, width), 1) <= iota((devices, width), 0), as_row, 0),
        axis=1, keepdims=True,
    )
    for q in range(pos.shape[0]):
        place_q = pos[q : q + 1, :]
        past = place_q >= ends
        source = jnp.sum(jnp.where(past, 1, 0), axis=0, keepdims=True)
        lo[q : q + 1, :] = place_q - jnp.sum(jnp.where(past, column, 0), axis=0, keepdims=True)
        hi[q : q + 1, :] = source * levels + level[...]

    def near_chunk(chunk, begin):
        size = ens.shape[0] // CHUNKS
        some = pl.ds(chunk * size, size)
        for index, turn in enumerate((1, -1)):
            exchange_pair(
                begin, *lat_has(n_lat, lat_at, turn),
                src_ref=ens.at[some], dst_ref=near.at[index, some],
                send_sem=near_send.at[index * CHUNKS + chunk],
                recv_sem=near_recv.at[index * CHUNKS + chunk],
                device_id=((lat_at + turn + n_lat) % n_lat, lon_at),
            )

    def side_copies(begin):
        for up, climb in enumerate((1, 0, -1)):
            for side, turn in enumerate((1, -1)):
                exchange_pair(
                    begin, *lat_has(n_lat, lat_at, climb),
                    src_ref=sides.at[pl.ds(side * half, half)],
                    dst_ref=near_sides.at[up, pl.ds(side * half, half)],
                    send_sem=side_send.at[up * 2 + side], recv_sem=side_recv.at[up * 2 + side],
                    device_id=(
                        (lat_at + climb + n_lat) % n_lat, (lon_at + turn + n_lon) % n_lon
                    ),
                )

    number = 2
    for iteration in range(iterations):
        before = iteration - 1
        if iteration > 0:
            send(lambda d: held.at[d % levels], field.at[before], number)
            field[before, me] = held[me % levels]
            if iteration == 1:
                make_sides(ens, sides)
                make_operators(
                    n_lat * rows, rows, cells, lat_taps, lon_taps, lat_op, lon_op,
                    lat_adjoint, lon_adjoint,
                )
                wait(whole, 1)
            wait(field.at[before], number)
            if iteration == 1:
                near_chunk(0, True)
                side_copies(True)
            covariance(
                n_lat, n_lon, coef, whole, field.at[before], lat_op, lon_op, part, wide, mid
            )
            send(lambda d: part.at[d], part_in.at[before], number + 1)
            part_in[before, me] = part[me]
            wait(part_in.at[before], number + 1)
            total = part_in[before, 0:levels]
            for g in range(1, devices // levels):
                total = total + part_in[before, g * levels : (g + 1) * levels]
            part[0:levels] = total
            if iteration == 1:
                near_chunk(1, True)
            to_slots(cols, part.at[0:levels], packed)
            send(lambda d: packed.at[d], table.at[before], number + 2)
            table[before, me] = packed[me]
            wait(table.at[before], number + 2)
            number += 3
            if iteration == 1:
                near_chunk(2, True)
                near_chunk(3, True)
        obs_step(
            table.at[before] if iteration > 0 else None,
            hi, lo, weight, innov, prec, departure, pushed, devices * levels, slots,
        )
        send(lambda d: pushed.at[d], incoming.at[iteration], number)
        if iteration == 0:
            send(members_of, whole, 1, early)
        incoming[iteration, me] = pushed[me]
        wait(incoming.at[iteration], number)
        number += 1
        forcing = to_columns(cols, incoming.at[iteration], held.shape)
        if iteration == 0:
            held[...] = -step[0] * forcing
        else:
            held[...] = held[...] - step[iteration] * (forcing + held[...])

    held_copies(n_lat, n_lon, lat_at, lon_at, held, near_held, held_send, held_recv, True)
    near_held[1, 1] = held[...]
    for chunk in range(CHUNKS):
        near_chunk(chunk, False)
    side_copies(False)
    held_copies(n_lat, n_lon, lat_at, lon_at, held, near_held, held_send, held_recv, False)


def exchange_pair(begin, has_send, has_recv, **copy):
    made = pltpu.make_async_remote_copy(device_id_type=MESH, **copy)
    if begin:
        pl.when(has_send)(made.start)
    else:
        pl.when(has_send)(made.wait_send)
        pl.when(has_recv)(made.wait_recv)


def lat_has(n_lat, lat_at, step):
    send = jnp.logical_and(lat_at + step >= 0, lat_at + step < n_lat)
    recv = jnp.logical_and(lat_at - step >= 0, lat_at - step < n_lat)
    return send, recv


def held_copies(n_lat, n_lon, lat_at, lon_at, held, near_held, held_send, held_recv, begin):
    for up, step in enumerate((1, 0, -1)):
        has = lat_has(n_lat, lat_at, step)
        for side, turn in enumerate((1, 0, -1)):
            if step == 0 and turn == 0:
                continue
            exchange_pair(
                begin, *has,
                src_ref=held, dst_ref=near_held.at[up, side],
                send_sem=held_send.at[up * 3 + side], recv_sem=held_recv.at[up * 3 + side],
                device_id=((lat_at + step + n_lat) % n_lat, (lon_at + turn + n_lon) % n_lon),
            )


def adjoint_kernel(scale, keep, members, near, edges, field, sigma, lon_op, lat_op, out, static_out):
    batch, levels, rows, cells = out.shape
    lon_high, lon_low = halves(lon_op[...])
    lat_high, lat_low = halves(lat_op[...])

    def smooth(pieces, count):
        stacked = jnp.concatenate(
            [piece.reshape(count, rows, 2 * cells) for piece in pieces], axis=1
        )
        group = lat_op.shape[0] // rows
        results = []
        for first in range(0, count, group):
            high, low = halves(
                stacked[first : first + group].reshape(group * 3 * rows, 2 * cells)
            )
            results.append(dot(lat_high, high) + dot(lat_low, high) + dot(lat_high, low))
        high, low = halves(jnp.concatenate(results, axis=0))
        return dot(high, lon_high) + dot(high, lon_low) + dot(low, lon_high)

    taken = edges.shape[1]
    place = jnp.where(iota((taken, cells), 0) == iota((taken, cells), 1), 1.0, 0.0).astype(BF16)
    count = batch * levels
    pieces = []
    for part in range(3):
        values = members[...] if part == 1 else near[part // 2]
        block = values.astype(F32) * field[part, :, :, :cells][None]
        edge = lax.dot_general(
            edges[part], place, (((0,), (0,)), ((), ())), preferred_element_type=F32
        ).reshape(out.shape)
        edge = edge * field[part, :, :, cells:][None]
        piece = jnp.concatenate([block, edge], axis=-1).reshape(count * rows, 2 * cells)
        pieces.append(piece if part == 1 else jnp.where(keep[part // 2] > 0, piece, 0.0))
    out[...] = scale * smooth(pieces, count).reshape(out.shape)

    @pl.when(pl.program_id(0) == 0)
    def _():
        pieces = [field[part].reshape(levels * rows, 2 * cells) for part in range(3)]
        static_out[...] = sigma[...] * smooth(pieces, levels).reshape(static_out.shape)


def divisor(count, limit):
    return max(n for n in range(1, count + 1) if count % n == 0 and (n <= limit or n == 1))


def per_device(
    ensemble,
    static_sigma,
    lat_taps,
    lon_taps,
    step_len,
    send_cols,
    send_count,
    obs_ref,
    obs_level,
    obs_weight,
    innovation,
    obs_precision,
):
    members, levels, rows, cells = ensemble.shape
    half = (lat_taps.shape[0] - 1) // 2
    n_lat, n_lon = lax.axis_size("lat"), lax.axis_size("lon")
    devices = n_lat * n_lon
    slots = send_cols.shape[3]
    scale = HYBRID_ENSEMBLE / math.sqrt(members - 1)
    lat_at = lax.axis_index("lat")
    lon_at = lax.axis_index("lon")

    positions = obs_ref.reshape(obs_ref.shape[2], -1)
    weight = obs_weight.reshape(positions.shape)
    groups = devices // levels
    per_group = members // groups
    device_at = lat_at * n_lon + lon_at
    level_at = device_at % levels

    wide_slots = max(slots, 256)
    cols = send_cols.reshape(-1, wide_slots)
    iterations = step_len.shape[0]
    lat_size = n_lat * rows * divisor(per_group + 1, max(1, 256 // (n_lat * rows)))
    side_shape = (2 * half, members * levels * rows)
    later = max(1, iterations - 1)
    fields = per_group + 1
    height = n_lat * rows
    static_coef = jnp.where(
        device_at < levels, HYBRID_STATIC**2 * static_sigma[level_at] ** 2, 0.0
    )
    coef = jnp.stack([static_coef, jnp.full((), scale * scale, F32)])
    count_width = -(-devices // 128) * 128
    count_row = jnp.pad(send_count.reshape(1, -1), ((0, 0), (0, count_width - devices)))
    smem = pl.BlockSpec(memory_space=pltpu.SMEM)
    hbm = pl.BlockSpec(memory_space=pl.ANY)
    exchanges = 2 + iterations + 3 * (iterations - 1)
    departure, near, near_sides, near_held, lat_adjoint, lon_adjoint = pl.pallas_call(
        functools.partial(main_kernel, n_lat, n_lon, iterations),
        out_shape=(
            jax.ShapeDtypeStruct((1, positions.shape[1]), F32),
            jax.ShapeDtypeStruct((2,) + ensemble.shape, BF16),
            jax.ShapeDtypeStruct((3,) + side_shape, BF16),
            jax.ShapeDtypeStruct((3, 3, levels, rows, cells), F32),
            jax.ShapeDtypeStruct((levels * rows, levels * 3 * rows), F32),
            jax.ShapeDtypeStruct((2 * cells, cells), F32),
        ),
        in_specs=[smem] * 4 + [VMEM] * 8,
        out_specs=(VMEM, hbm, VMEM, VMEM, VMEM, VMEM),
        scratch_shapes=[
            pltpu.VMEM((devices, 1, count_width), jnp.int32),
            pltpu.VMEM((devices, per_group, rows, cells), BF16),
            pltpu.VMEM((devices, levels, slots), F32),
            pltpu.VMEM((iterations, devices, levels, slots), F32),
            pltpu.VMEM((later, devices, rows, cells), F32),
            pltpu.VMEM((devices, rows, cells), F32),
            pltpu.VMEM((later, devices, rows, cells), F32),
            pltpu.VMEM((devices, levels, slots), F32),
            pltpu.VMEM((later, devices, levels, slots), F32),
            pltpu.VMEM((levels, rows, cells), F32),
            pltpu.VMEM((fields * height, (n_lon + 2) * cells), F32),
            pltpu.VMEM((fields * height, n_lon * cells), F32),
            pltpu.VMEM(positions.shape, jnp.int32),
            pltpu.VMEM(positions.shape, jnp.int32),
            pltpu.VMEM(side_shape, BF16),
            pltpu.VMEM((lat_size, lat_size), F32),
            pltpu.VMEM((3 * cells, cells), F32),
            pltpu.SemaphoreType.DMA((exchanges,)),
            pltpu.SemaphoreType.DMA((exchanges,)),
            pltpu.SemaphoreType.DMA((2 * CHUNKS,)),
            pltpu.SemaphoreType.DMA((2 * CHUNKS,)),
            pltpu.SemaphoreType.DMA((6,)),
            pltpu.SemaphoreType.DMA((6,)),
            pltpu.SemaphoreType.DMA((9,)),
            pltpu.SemaphoreType.DMA((9,)),
        ],
        compiler_params=pltpu.CompilerParams(collective_id=0, has_side_effects=True),
        name="analysis",
    )(
        coef, step_len, lat_taps, lon_taps, ensemble, count_row, cols, positions,
        obs_level.reshape(1, -1), weight, innovation.reshape(1, -1),
        obs_precision.reshape(1, -1),
    )
    wide3 = jnp.concatenate(
        [
            near_held[:, 1],
            near_held[:, 0, :, :, cells - half :],
            near_held[:, 2, :, :, :half],
            jnp.zeros((3, levels, rows, cells - 2 * half), F32),
        ],
        axis=3,
    )
    keep = jnp.stack([lat_at > 0, lat_at < n_lat - 1]).astype(jnp.int32)
    wide3 = jnp.where(
        jnp.stack([keep[0], jnp.ones((), jnp.int32), keep[1]])[:, None, None, None] > 0, wide3, 0.0
    )
    batch = divisor(members, 8)
    sigma = jnp.broadcast_to(
        (HYBRID_STATIC * static_sigma)[:, None, None], (levels, rows, cells)
    )
    own_spec = pl.BlockSpec((batch, levels, rows, cells), lambda k: (k, 0, 0, 0))
    near_spec = pl.BlockSpec((2, batch, levels, rows, cells), lambda k: (0, k, 0, 0, 0))
    edge_spec = pl.BlockSpec((3, 2 * half, batch * levels * rows), lambda k: (0, 0, k))
    control, static = pl.pallas_call(
        functools.partial(adjoint_kernel, scale),
        grid=(members // batch,),
        out_shape=(
            jax.ShapeDtypeStruct(ensemble.shape, F32),
            jax.ShapeDtypeStruct((levels, rows, cells), F32),
        ),
        in_specs=[smem, own_spec, near_spec, edge_spec] + [VMEM] * 4,
        out_specs=(
            pl.BlockSpec((batch, levels, rows, cells), lambda k: (k, 0, 0, 0)),
            pl.BlockSpec((levels, rows, cells), lambda k: (0, 0, 0)),
        ),
        name="adjoint",
    )(keep, ensemble, near, near_sides, wide3, sigma, lon_adjoint, lat_adjoint)
    return control, static, departure.reshape(1, 1, -1)


def solution(mesh):
    return jax.shard_map(
        per_device,
        mesh=mesh,
        in_specs=(
            P(None, None, "lat", "lon"),
            P(),
            P(),
            P(),
            P(),
            P("lat", "lon", None, None),
            P("lat", "lon", None),
            P("lat", "lon", None, None),
            P("lat", "lon", None),
            P("lat", "lon", None, None),
            P("lat", "lon", None),
            P("lat", "lon", None),
        ),
        out_specs=(P(None, None, "lat", "lon"), P(None, "lat", "lon"), P("lat", "lon", None)),
        check_vma=False,
    )
```
